32 devices in a mesh: groups: 2 (over y), seq: 4 (over z), mp: 4 (over x, core).
Axes of the slice: x: 2, y: 2, z: 4, core: 2. Of those that a mesh axis runs over, the one named last changes fastest.
Arguments:
- node_vectors: bfloat16 [1024, 2048], P(('groups', 'seq'), 'mp'), parts along dimension 0, may hold values from -6 to 6
- standardize_multiplier: float32 [2048], replicated, may hold values from 0.1 to 1.9
- probe_matrix: bfloat16 [2048, 1024], P(None, 'mp'), may hold values from -1 to 1
- lookup_matrix: bfloat16 [2048, 1024], P(None, 'mp'), may hold values from -1 to 1
- content_matrix: bfloat16 [2048, 1024], P(None, 'mp'), may hold values from -0.125 to 0.125
- softness_per_group: float32 [8], P('mp'), may hold values from 0.5 to 12
- exit_matrix: bfloat16 [1024, 2048], P('mp'), may hold values from -0.1875 to 0.1875
Outputs:
- mixed: bfloat16 [1024, 2048], P(('groups', 'seq'), 'mp'), parts along dimension 0
The draws below stay inside these ranges and needn't reach their ends.
There are 2 independent parts, one for each index of `groups`. The reference program is written for one: setup_inputs(seed, part) draws one part's arguments, and reference() takes and returns one part's arrays. A program takes and returns all parts, laid end to end along the dimension named above; an argument that names none is the same for every part. Nothing has to cross between parts.
All inputs are finite; a program needn't handle non-finite values.
Results may differ from the reference program's by a relative error of at most 0.011.
Values may be sent and summed in bfloat16 or wider, within the bound.
A program may use at most 64 MiB of HBM per device.

```python
import math
import jax
import jax.numpy as jnp
from jax import lax

D = 2048
HEADS = 8
CHANNEL_SPAN = 128
LENGTH = 512


def draw_node_vectors(key, part):
    drawn = jax.random.normal(jax.random.fold_in(key, 21), (LENGTH, D), jnp.float32)
    return jnp.clip(drawn, -6.0, 6.0).astype(jnp.bfloat16)


def query_matrix(key):
    return jax.random.normal(jax.random.fold_in(key, 31), (D, HEADS * CHANNEL_SPAN), jnp.float32) / math.sqrt(D)


def draw_probe_matrix(key, part):
    return jnp.clip(query_matrix(key), -1.0, 1.0).astype(jnp.bfloat16)


def draw_lookup_matrix(key, part):
    drawn = jax.random.normal(jax.random.fold_in(key, 32), (D, HEADS * CHANNEL_SPAN), jnp.float32) / math.sqrt(D)
    return jnp.clip(drawn, -1.0, 1.0).astype(jnp.bfloat16)


def draw_softness_per_group(key, part):
    uniform_draw = jax.random.uniform(jax.random.fold_in(key, 41), (HEADS,), jnp.float32)
    return jnp.power(4.0, uniform_draw)


def block_scale(own_key, dims, shards, smallest, top_value):
    loudness = 1.0
    for dim, parts in shards:
        steps = jax.random.uniform(jax.random.fold_in(jax.random.fold_in(own_key, 6), dim), (parts,), jnp.float32, smallest / len(shards), top_value / len(shards))
        loudness = loudness * jnp.repeat(jnp.exp(steps), dims[dim] // parts).reshape((-1,) + (1,) * (len(dims) - 1 - dim))
    return loudness


def scatter_about(stream_key, shape, width, most, cuts=(), dtype=jnp.bfloat16):
    entries = jax.random.normal(stream_key, shape, jnp.float32) * width
    if len(cuts) > 0:
        entries = block_scale(stream_key, shape, cuts, -0.22, 0.18) * entries
    return jnp.clip(entries, min=-most, max=most).astype(dtype)


def setup_inputs(seed: int = 0, part: int = 0) -> dict:
    key_list = jax.random.split(jax.random.key(seed), 8)
    own_keys = jax.random.split(jax.random.fold_in(key_list[7], part), 8)
    node_vectors = draw_node_vectors(jax.random.fold_in(jax.random.fold_in(key_list[7], part), 71), part)
    standardize_multiplier = jnp.clip(1.0 + 0.18 * jax.random.normal(key_list[1], (D,), jnp.float32), 0.1, 1.9)
    probe_matrix = draw_probe_matrix(jax.random.fold_in(key_list[7], 71), part)
    lookup_matrix = draw_lookup_matrix(jax.random.fold_in(key_list[7], 71), part)
    content_matrix = scatter_about(key_list[4], (D, HEADS * CHANNEL_SPAN), D ** -0.5, 0.125, ((1, 4),))
    softness_per_group = draw_softness_per_group(jax.random.fold_in(key_list[7], 71), part)
    exit_matrix = scatter_about(key_list[6], (HEADS * CHANNEL_SPAN, D), (HEADS * CHANNEL_SPAN) ** -0.5, 0.1875, ((0, 4),))
    return dict(node_vectors=node_vectors, standardize_multiplier=standardize_multiplier, probe_matrix=probe_matrix, lookup_matrix=lookup_matrix, content_matrix=content_matrix, softness_per_group=softness_per_group, exit_matrix=exit_matrix)


def reference(node_vectors, standardize_multiplier, probe_matrix, lookup_matrix, content_matrix, softness_per_group, exit_matrix):
    widened = node_vectors.astype(jnp.float32)
    average = lax.optimization_barrier(jnp.mean(widened, axis=-1, keepdims=True))
    centered = widened - average
    variance = lax.optimization_barrier(jnp.mean(centered * centered, axis=-1, keepdims=True))
    normed = (centered * lax.rsqrt(variance + 1e-05) * standardize_multiplier).astype(jnp.bfloat16)
    queries = jnp.dot(normed, probe_matrix, preferred_element_type=jnp.float32).astype(jnp.bfloat16)
    key_rows = jnp.dot(normed, lookup_matrix, preferred_element_type=jnp.float32).astype(jnp.bfloat16)
    value_rows = jnp.dot(normed, content_matrix, preferred_element_type=jnp.float32).astype(jnp.bfloat16)
    query_heads = queries.reshape(LENGTH, HEADS, CHANNEL_SPAN).transpose(1, 0, 2)
    key_heads = key_rows.reshape(LENGTH, HEADS, CHANNEL_SPAN).transpose(1, 0, 2)
    value_heads = value_rows.reshape(LENGTH, HEADS, CHANNEL_SPAN).transpose(1, 0, 2)
    inverse_root_span = softness_per_group / math.sqrt(CHANNEL_SPAN)
    block_rows = math.gcd(LENGTH, 1024)

    def one_head(inputs):
        head_queries, head_keys, head_values, head_factor = inputs

        def one_block(query_block):
            scores = jnp.dot(query_block, head_keys.T, preferred_element_type=jnp.float32) * head_factor
            row_max = lax.optimization_barrier(jnp.max(scores, axis=-1, keepdims=True))
            weights = jnp.exp(scores - row_max)
            totals = lax.optimization_barrier(jnp.sum(weights, axis=-1, keepdims=True))
            attended = jnp.dot(weights.astype(jnp.bfloat16), head_values, preferred_element_type=jnp.float32)
            return attended / totals
        blocks = head_queries.reshape(LENGTH // block_rows, block_rows, CHANNEL_SPAN)
        return lax.map(one_block, blocks).reshape(LENGTH, CHANNEL_SPAN)
    attended = lax.map(one_head, (query_heads, key_heads, value_heads, inverse_root_span))
    heads_out = attended.transpose(1, 0, 2).reshape(LENGTH, HEADS * CHANNEL_SPAN).astype(jnp.bfloat16)
    projected = jnp.dot(heads_out, exit_matrix, preferred_element_type=jnp.float32)
    return (widened + projected).astype(jnp.bfloat16)
```

```python
import functools
import math

import jax
import jax.numpy as jnp
from jax import lax
from jax.experimental import pallas as pl
from jax.experimental.pallas import tpu as pltpu
from jax.sharding import PartitionSpec as P

MESH = pl.DeviceIdType.MESH
F32 = jnp.float32
BF16 = jnp.bfloat16
UNROLL_LIMIT = 8


def remote(src, dst, send_sem, recv_sem, axis, index):
    return pltpu.make_async_remote_copy(
        src_ref=src,
        dst_ref=dst,
        send_sem=send_sem,
        recv_sem=recv_sem,
        device_id={axis: index},
        device_id_type=MESH,
    )


def each(count, body):
    if count <= UNROLL_LIMIT:
        for i in range(count):
            body(i)
    else:
        lax.fori_loop(0, count, lambda i, c: (body(i), c)[1], 0)


def kernel(
    n_mp,
    n_seq,
    softness_ref,
    x_hbm,
    gain_ref,
    wq_hbm,
    wk_hbm,
    wv_hbm,
    wo_hbm,
    out_ref,
    xg,
    wq,
    wk,
    wv,
    wo,
    normed,
    q_ref,
    kv,
    scores,
    heads,
    out_send,
    out_recv,
    w_sem,
    x_sem,
    xg_send,
    xg_recv,
    kv_send,
    kv_recv,
    rs_send,
    rs_recv,
):
    me = lax.axis_index("mp")
    spot = lax.axis_index("seq")
    rows, part = x_hbm.shape
    head_cols = wq_hbm.shape[1]
    groups = softness_ref.shape[0]
    span = head_cols // groups
    paired = n_mp == 4
    has_left = spot > 0
    has_right = spot < n_seq - 1

    own_x = pltpu.make_async_copy(x_hbm, xg.at[me], x_sem)
    own_x.start()
    loads = [
        pltpu.make_async_copy(src, dst, w_sem.at[i])
        for i, (src, dst) in enumerate(((wk_hbm, wk), (wv_hbm, wv), (wq_hbm, wq), (wo_hbm, wo)))
    ]
    for load in loads:
        load.start()

    barrier = pltpu.get_barrier_semaphore()
    for step in range(1, n_mp):
        pl.semaphore_signal(
            barrier, inc=1, device_id={"mp": lax.rem(me + step, n_mp)}, device_id_type=MESH
        )

    @pl.when(has_left)
    def _():
        pl.semaphore_signal(barrier, inc=1, device_id={"seq": spot - 1}, device_id_type=MESH)

    @pl.when(has_right)
    def _():
        pl.semaphore_signal(barrier, inc=1, device_id={"seq": spot + 1}, device_id_type=MESH)

    pl.semaphore_wait(
        barrier, n_mp - 1 + has_left.astype(jnp.int32) + has_right.astype(jnp.int32)
    )

    if paired:
        near = me + 1 - 2 * lax.rem(me, 2)
        far = lax.rem(me + 2, 4)
        cross = lax.rem(near + 2, 4)
        half = rows // 2
        pieces = [pl.ds(0, half), pl.ds(half, half)]
        sends = []
        for c, piece in enumerate(pieces):
            sends.append(
                remote(x_hbm.at[piece], xg.at[me, piece], xg_send.at[0, c], xg_recv.at[0, c], "mp", far)
            )
        for c, piece in enumerate(pieces):
            sends.append(
                remote(x_hbm.at[piece], xg.at[me, piece], xg_send.at[1, c], xg_recv.at[1, c], "mp", near)
            )
        for send in sends:
            send.start()
        for c, piece in enumerate(pieces):
            remote(
                xg.at[far, piece], xg.at[far, piece], xg_send.at[0, c], xg_recv.at[0, c], "mp", far
            ).wait_recv()
            relay = remote(
                xg.at[far, piece], xg.at[far, piece], xg_send.at[2, c], xg_recv.at[2, c], "mp", near
            )
            relay.start()
            sends.append(relay)
        for c, piece in enumerate(pieces):
            remote(
                xg.at[near, piece], xg.at[near, piece], xg_send.at[1, c], xg_recv.at[1, c], "mp", near
            ).wait_recv()
        for c, piece in enumerate(pieces):
            remote(
                xg.at[cross, piece], xg.at[cross, piece], xg_send.at[2, c], xg_recv.at[2, c], "mp", near
            ).wait_recv()
    else:
        sends = []
        for step in range(1, n_mp):
            peer = lax.rem(me + step, n_mp)
            send = remote(
                x_hbm, xg.at[me], xg_send.at[step, 0], xg_recv.at[step, 0], "mp", peer
            )
            send.start()
            sends.append(send)
        for step in range(1, n_mp):
            source = lax.rem(me - step + n_mp, n_mp)
            remote(
                xg.at[source], xg.at[source], xg_send.at[step, 0], xg_recv.at[step, 0], "mp", source
            ).wait_recv()
    own_x.wait()

    features = n_mp * part
    total = jnp.zeros((rows, 1), F32)
    for j in range(n_mp):
        total = total + jnp.sum(xg[j].astype(F32), axis=-1, keepdims=True)
    average = total / features
    square = jnp.zeros((rows, 1), F32)
    for j in range(n_mp):
        off = xg[j].astype(F32) - average
        square = square + jnp.sum(off * off, axis=-1, keepdims=True)
    inverse = lax.rsqrt(square / features + 1e-05)
    for j in range(n_mp):
        cols = pl.ds(j * part, part)
        off = xg[j].astype(F32) - average
        normed[:, cols] = (off * inverse * gain_ref[:, cols]).astype(BF16)

    for which, (load, weight) in enumerate(((loads[0], wk), (loads[1], wv))):
        load.wait()
        kv[which, spot] = jnp.dot(
            normed[...], weight[...], preferred_element_type=F32
        ).astype(BF16)

        @pl.when(has_right)
        def _():
            remote(
                kv.at[which, spot], kv.at[which, spot],
                kv_send.at[1, which, spot], kv_recv.at[which, spot], "seq", spot + 1,
            ).start()

        @pl.when(has_left)
        def _():
            remote(
                kv.at[which, spot], kv.at[which, spot],
                kv_send.at[0, which, spot], kv_recv.at[which, spot], "seq", spot - 1,
            ).start()

    loads[2].wait()
    q_ref[...] = jnp.dot(normed[...], wq[...], preferred_element_type=F32).astype(BF16)

    def arrive(which, step):
        before = spot - step
        after = spot + step

        @pl.when(before >= 0)
        def _():
            remote(
                kv.at[which, before], kv.at[which, before],
                kv_send.at[1, which, before], kv_recv.at[which, before], "seq", spot - 1,
            ).wait_recv()

            @pl.when(has_right)
            def _():
                remote(
                    kv.at[which, before], kv.at[which, before],
                    kv_send.at[1, which, before], kv_recv.at[which, before], "seq", spot + 1,
                ).start()

        @pl.when(after < n_seq)
        def _():
            remote(
                kv.at[which, after], kv.at[which, after],
                kv_send.at[0, which, after], kv_recv.at[which, after], "seq", spot + 1,
            ).wait_recv()

            @pl.when(has_left)
            def _():
                remote(
                    kv.at[which, after], kv.at[which, after],
                    kv_send.at[0, which, after], kv_recv.at[which, after], "seq", spot - 1,
                ).start()

    def both(i):
        arrive(0, i + 1)
        arrive(1, i + 1)

    if n_seq > 2:
        each(n_seq - 2, both)
    if n_seq > 1:
        arrive(0, n_seq - 1)

    if n_seq <= UNROLL_LIMIT:
        sums, chances = [], []
        for h in range(groups):
            cols = pl.ds(h * span, span)
            keys = kv[0, :, :, cols].reshape(n_seq * rows, span)
            s = lax.dot_general(
                q_ref[:, cols], keys, (((1,), (1,)), ((), ())), preferred_element_type=F32
            ) * (softness_ref[h] / math.sqrt(span))
            top = jnp.max(s, axis=-1, keepdims=True)
            w = jnp.exp(s - top)
            sums.append(jnp.sum(w, axis=-1, keepdims=True))
            chances.append(w.astype(BF16))
        if n_seq > 1:
            arrive(1, n_seq - 1)
        for h in range(groups):
            cols = pl.ds(h * span, span)
            values = kv[1, :, :, cols].reshape(n_seq * rows, span)
            mixed = jnp.dot(chances[h], values, preferred_element_type=F32)
            heads[:, cols] = (mixed / sums[h]).astype(BF16)
    else:
        arrive(1, n_seq - 1)
        for h in range(groups):
            cols = pl.ds(h * span, span)
            factor = softness_ref[h] / math.sqrt(span)

            def first(b, top):
                s = lax.dot_general(
                    q_ref[:, cols], kv[0, b, :, cols], (((1,), (1,)), ((), ())),
                    preferred_element_type=F32,
                ) * factor
                scores[b] = s
                return jnp.maximum(top, jnp.max(s, axis=-1, keepdims=True))

            top = lax.fori_loop(0, n_seq, first, jnp.full((rows, 1), -jnp.inf, F32))

            def second(b, state):
                summed, mixed = state
                w = jnp.exp(scores[b] - top)
                mixed = mixed + jnp.dot(
                    w.astype(BF16), kv[1, b, :, cols], preferred_element_type=F32
                )
                return summed + jnp.sum(w, axis=-1, keepdims=True), mixed

            summed, mixed = lax.fori_loop(
                0, n_seq, second, (jnp.zeros((rows, 1), F32), jnp.zeros((rows, span), F32))
            )
            heads[:, cols] = (mixed / summed).astype(BF16)

    loads[3].wait()

    def share(owner):
        cols = pl.ds(pl.multiple_of(owner * part, part), part)
        return jnp.dot(heads[...], wo[:, cols], preferred_element_type=F32)

    if paired:
        out_send[0] = share(cross).astype(BF16)
        first = remote(out_send.at[0], out_recv.at[0], rs_send.at[0], rs_recv.at[0], "mp", near)
        first.start()
        for_far = share(far)
        out_send[1] = share(near).astype(BF16)
        second = remote(out_send.at[1], out_recv.at[1], rs_send.at[1], rs_recv.at[1], "mp", near)
        second.start()
        first.wait_recv()
        out_send[2] = (for_far + out_recv[0].astype(F32)).astype(BF16)
        third = remote(out_send.at[2], out_recv.at[2], rs_send.at[2], rs_recv.at[2], "mp", far)
        third.start()
        own = share(me) + xg[me].astype(F32)
        second.wait_recv()
        own = own + out_recv[1].astype(F32)
        third.wait_recv()
        out_ref[...] = (own + out_recv[2].astype(F32)).astype(BF16)
        sends.extend((first, second, third))
    else:
        for step in range(1, n_mp):
            peer = lax.rem(me + step, n_mp)
            out_send[step] = share(peer).astype(BF16)
            send = remote(
                out_send.at[step], out_recv.at[step], rs_send.at[step], rs_recv.at[step], "mp", peer
            )
            send.start()
            sends.append(send)
        own = share(me) + xg[me].astype(F32)
        for step in range(1, n_mp):
            remote(
                out_send.at[step], out_recv.at[step], rs_send.at[step], rs_recv.at[step], "mp", me
            ).wait_recv()
            own = own + out_recv[step].astype(F32)
        out_ref[...] = own.astype(BF16)

    for send in sends:
        send.wait_send()

    def drain(b):
        for which in range(2):

            @pl.when(has_right & (b <= spot))
            def _():
                remote(
                    kv.at[which, b], kv.at[which, b],
                    kv_send.at[1, which, b], kv_recv.at[which, b], "seq", spot + 1,
                ).wait_send()

            @pl.when(has_left & (b >= spot))
            def _():
                remote(
                    kv.at[which, b], kv.at[which, b],
                    kv_send.at[0, which, b], kv_recv.at[which, b], "seq", spot - 1,
                ).wait_send()

    each(n_seq, drain)


def per_device(n_mp, n_seq, x, gain, wq, wk, wv, softness, wo):
    rows, part = x.shape
    features, head_cols = wq.shape
    span_rows = n_seq if n_seq > UNROLL_LIMIT else 1
    any_space = pl.BlockSpec(memory_space=pl.ANY)
    vmem = pl.BlockSpec(memory_space=pltpu.VMEM)
    slots = max(n_mp, 3)
    return pl.pallas_call(
        functools.partial(kernel, n_mp, n_seq),
        out_shape=jax.ShapeDtypeStruct((rows, part), BF16),
        in_specs=[
            pl.BlockSpec(memory_space=pltpu.SMEM),
            any_space, vmem, any_space, any_space, any_space, any_space,
        ],
        out_specs=vmem,
        scratch_shapes=[
            pltpu.VMEM((n_mp, rows, part), BF16),
            pltpu.VMEM((features, head_cols), BF16),
            pltpu.VMEM((features, head_cols), BF16),
            pltpu.VMEM((features, head_cols), BF16),
            pltpu.VMEM((head_cols, features), BF16),
            pltpu.VMEM((rows, features), BF16),
            pltpu.VMEM((rows, head_cols), BF16),
            pltpu.VMEM((2, n_seq, rows, head_cols), BF16),
            pltpu.VMEM((span_rows, rows, rows), F32),
            pltpu.VMEM((rows, head_cols), BF16),
            pltpu.VMEM((slots, rows, part), BF16),
            pltpu.VMEM((slots, rows, part), BF16),
            pltpu.SemaphoreType.DMA((4,)),
            pltpu.SemaphoreType.DMA,
            pltpu.SemaphoreType.DMA((slots, 2)),
            pltpu.SemaphoreType.DMA((slots, 2)),
            pltpu.SemaphoreType.DMA((2, 2, n_seq)),
            pltpu.SemaphoreType.DMA((2, n_seq)),
            pltpu.SemaphoreType.DMA((slots,)),
            pltpu.SemaphoreType.DMA((slots,)),
        ],
        compiler_params=pltpu.CompilerParams(collective_id=0, has_side_effects=True),
    )(softness, x, gain.reshape(1, features), wq, wk, wv, wo)


def solution(mesh):
    return jax.shard_map(
        functools.partial(per_device, mesh.shape["mp"], mesh.shape["seq"]),
        mesh=mesh,
        in_specs=(
            P(("groups", "seq"), "mp"),
            P(),
            P(None, "mp"),
            P(None, "mp"),
            P(None, "mp"),
            P("mp"),
            P("mp", None),
        ),
        out_specs=P(("groups", "seq"), "mp"),
        check_vma=False,
    )
```

```python
import functools
import math

import jax
import jax.numpy as jnp
from jax import lax
from jax.experimental import pallas as pl
from jax.experimental.pallas import tpu as pltpu
from jax.sharding import PartitionSpec as P

MESH = pl.DeviceIdType.MESH
F32 = jnp.float32
BF16 = jnp.bfloat16
UNROLL_LIMIT = 8
RS_PIECES = 4


def remote(src, dst, send_sem, recv_sem, axis, index):
    return pltpu.make_async_remote_copy(
        src_ref=src,
        dst_ref=dst,
        send_sem=send_sem,
        recv_sem=recv_sem,
        device_id={axis: index},
        device_id_type=MESH,
    )


def each(count, body):
    if count <= UNROLL_LIMIT:
        for i in range(count):
            body(i)
    else:
        lax.fori_loop(0, count, lambda i, c: (body(i), c)[1], 0)


def kernel(
    n_mp,
    n_seq,
    softness_ref,
    x_hbm,
    gain_ref,
    wq_hbm,
    wk_hbm,
    wv_hbm,
    wo_hbm,
    out_ref,
    xg,
    wq,
    wk,
    wv,
    wo,
    normed,
    q_ref,
    kv,
    scores,
    heads,
    out_send,
    out_recv,
    w_sem,
    x_sem,
    xg_send,
    xg_recv,
    kv_send,
    kv_recv,
    rs_send,
    rs_recv,
):
    me = lax.axis_index("mp")
    spot = lax.axis_index("seq")
    rows, part = x_hbm.shape
    head_cols = wq_hbm.shape[1]
    groups = softness_ref.shape[0]
    span = head_cols // groups
    paired = n_mp == 4
    has_left = spot > 0
    has_right = spot < n_seq - 1
    hop = n_seq == 4
    ends = (spot == 0) | (spot == n_seq - 1)

    own_x = pltpu.make_async_copy(x_hbm, xg.at[me], x_sem)
    own_x.start()
    loads = [
        pltpu.make_async_copy(src, dst, w_sem.at[i])
        for i, (src, dst) in enumerate(((wk_hbm, wk), (wv_hbm, wv), (wq_hbm, wq), (wo_hbm, wo)))
    ]
    for load in loads:
        load.start()

    barrier = pltpu.get_barrier_semaphore()
    for step in range(1, n_mp):
        pl.semaphore_signal(
            barrier, inc=1, device_id={"mp": lax.rem(me + step, n_mp)}, device_id_type=MESH
        )

    @pl.when(has_left)
    def _():
        pl.semaphore_signal(barrier, inc=1, device_id={"seq": spot - 1}, device_id_type=MESH)

    @pl.when(has_right)
    def _():
        pl.semaphore_signal(barrier, inc=1, device_id={"seq": spot + 1}, device_id_type=MESH)

    greeted = n_mp - 1 + has_left.astype(jnp.int32) + has_right.astype(jnp.int32)
    if hop:

        @pl.when(ends)
        def _():
            pl.semaphore_signal(
                barrier, inc=1, device_id={"seq": n_seq - 1 - spot}, device_id_type=MESH
            )

        greeted = greeted + ends.astype(jnp.int32)
    pl.semaphore_wait(barrier, greeted)

    half = rows // 2
    pieces = [pl.ds(0, half), pl.ds(half, half)]
    near = me + 1 - 2 * lax.rem(me, 2)
    far = lax.rem(me + 2, n_mp)
    cross = lax.rem(near + 2, n_mp)
    sends = []

    def gather(lane, c, source, target):
        slot = xg.at[source, pieces[c]]
        return remote(slot, slot, xg_send.at[lane, c], xg_recv.at[lane, c], "mp", target)

    if paired:
        for lane, peer in ((0, far), (1, near)):
            for c, piece in enumerate(pieces):
                send = remote(
                    x_hbm.at[piece], xg.at[me, piece],
                    xg_send.at[lane, c], xg_recv.at[lane, c], "mp", peer,
                )
                send.start()
                sends.append(send)
    else:
        for c, piece in enumerate(pieces):
            for step in range(1, n_mp):
                send = remote(
                    x_hbm.at[piece], xg.at[me, piece],
                    xg_send.at[step, c], xg_recv.at[step, c], "mp", lax.rem(me + step, n_mp),
                )
                send.start()
                sends.append(send)
    own_x.wait()

    def relay_far(c):
        if paired:
            gather(0, c, far, far).wait_recv()
            relay = gather(2, c, far, near)
            relay.start()
            sends.append(relay)

    def gathered(c):
        if paired:
            gather(1, c, near, near).wait_recv()
            gather(2, c, cross, near).wait_recv()
        else:
            for step in range(1, n_mp):
                source = lax.rem(me - step + n_mp, n_mp)
                gather(step, c, source, source).wait_recv()

    features = n_mp * part

    def normalize(c):
        piece = pieces[c]
        total = jnp.zeros((half, 1), F32)
        for j in range(n_mp):
            total = total + jnp.sum(xg[j, piece, :].astype(F32), axis=-1, keepdims=True)
        average = total / features
        square = jnp.zeros((half, 1), F32)
        for j in range(n_mp):
            off = xg[j, piece, :].astype(F32) - average
            square = square + jnp.sum(off * off, axis=-1, keepdims=True)
        inverse = lax.rsqrt(square / features + 1e-05)
        for j in range(n_mp):
            cols = pl.ds(j * part, part)
            off = xg[j, piece, :].astype(F32) - average
            normed[piece, cols] = (off * inverse * gain_ref[:, cols]).astype(BF16)

    def block(way, which, owner, c, target):
        slot = kv.at[which, owner, pieces[c]]
        return remote(
            slot, slot, kv_send.at[way, which, owner, c], kv_recv.at[which, owner, c], "seq", target
        )

    def project(which, weight, c):
        kv[which, spot, pieces[c]] = jnp.dot(
            normed[pieces[c], :], weight[...], preferred_element_type=F32
        ).astype(BF16)

        @pl.when(has_right)
        def _():
            block(1, which, spot, c, spot + 1).start()

        @pl.when(has_left)
        def _():
            block(0, which, spot, c, spot - 1).start()

        if hop:

            @pl.when(ends)
            def _():
                block(2, which, spot, c, n_seq - 1 - spot).start()

    relay_far(0)
    gathered(0)
    normalize(0)
    relay_far(1)
    for which, weight in ((0, wk), (1, wv)):
        loads[which].wait()
        project(which, weight, 0)
    gathered(1)
    normalize(1)
    for which, weight in ((0, wk), (1, wv)):
        project(which, weight, 1)
    loads[2].wait()
    q_ref[...] = jnp.dot(normed[...], wq[...], preferred_element_type=F32).astype(BF16)

    def take(which, step, c, forward):
        before = spot - step
        after = spot + step

        @pl.when(before >= 0)
        def _():
            block(1, which, before, c, before).wait_recv()
            if forward:

                @pl.when(has_right)
                def _():
                    block(1, which, before, c, spot + 1).start()

        @pl.when(after < n_seq)
        def _():
            block(0, which, after, c, after).wait_recv()
            if forward:

                @pl.when(has_left)
                def _():
                    block(0, which, after, c, spot - 1).start()

    if hop:
        for c in range(2):
            for which in range(2):
                take(which, 1, c, True)
        for step in (2, 3):
            for c in range(2):
                take(0, step, c, False)

        def last_values():
            for step in (2, 3):
                for c in range(2):
                    take(1, step, c, False)

    else:

        def chain(i):
            for c in range(2):
                for which in range(2):
                    take(which, i + 1, c, True)

        each(n_seq - 1, chain)

        def last_values():
            pass

    if n_seq <= UNROLL_LIMIT:
        sums, chances = [], []
        for h in range(groups):
            cols = pl.ds(h * span, span)
            keys = kv[0, :, :, cols].reshape(n_seq * rows, span)
            s = lax.dot_general(
                q_ref[:, cols], keys, (((1,), (1,)), ((), ())), preferred_element_type=F32
            ) * (softness_ref[h] / math.sqrt(span))
            top = jnp.max(s, axis=-1, keepdims=True)
            w = jnp.exp(s - top)
            sums.append(jnp.sum(w, axis=-1, keepdims=True))
            chances.append(w.astype(BF16))
        last_values()
        for h in range(groups):
            cols = pl.ds(h * span, span)
            values = kv[1, :, :, cols].reshape(n_seq * rows, span)
            mixed = jnp.dot(chances[h], values, preferred_element_type=F32)
            heads[:, cols] = (mixed / sums[h]).astype(BF16)
    else:
        for h in range(groups):
            cols = pl.ds(h * span, span)
            factor = softness_ref[h] / math.sqrt(span)

            def first(b, top):
                s = lax.dot_general(
                    q_ref[:, cols], kv[0, b, :, cols], (((1,), (1,)), ((), ())),
                    preferred_element_type=F32,
                ) * factor
                scores[b] = s
                return jnp.maximum(top, jnp.max(s, axis=-1, keepdims=True))

            top = lax.fori_loop(0, n_seq, first, jnp.full((rows, 1), -jnp.inf, F32))

            def second(b, state):
                summed, mixed = state
                w = jnp.exp(scores[b] - top)
                mixed = mixed + jnp.dot(
                    w.astype(BF16), kv[1, b, :, cols], preferred_element_type=F32
                )
                return summed + jnp.sum(w, axis=-1, keepdims=True), mixed

            summed, mixed = lax.fori_loop(
                0, n_seq, second, (jnp.zeros((rows, 1), F32), jnp.zeros((rows, span), F32))
            )
            heads[:, cols] = (mixed / summed).astype(BF16)

    loads[3].wait()
    rs_pieces = [pl.ds(i * (rows // RS_PIECES), rows // RS_PIECES) for i in range(RS_PIECES)]

    def share(owner):
        cols = pl.ds(pl.multiple_of(owner * part, part), part)
        return jnp.dot(heads[...], wo[:, cols], preferred_element_type=F32)

    if paired:
        quarter = rows // len(rs_pieces)

        def reduce(lane, piece, target):
            return remote(
                out_send.at[lane, piece], out_recv.at[lane, piece],
                rs_send.at[lane, piece.start // quarter], rs_recv.at[lane, piece.start // quarter],
                "mp", target,
            )

        out_send[0] = share(cross).astype(BF16)
        for piece in rs_pieces:
            send = reduce(0, piece, near)
            send.start()
            sends.append(send)
        for_far = share(far)
        for piece in rs_pieces:
            reduce(0, piece, near).wait_recv()
            low = piece.start
            out_send[2, piece] = (
                for_far[low : low + quarter] + out_recv[0, piece].astype(F32)
            ).astype(BF16)
            send = reduce(2, piece, far)
            send.start()
            sends.append(send)
        out_send[1] = share(near).astype(BF16)
        for piece in rs_pieces:
            send = reduce(1, piece, near)
            send.start()
            sends.append(send)
        own = share(me) + xg[me].astype(F32)
        for piece in rs_pieces:
            reduce(1, piece, near).wait_recv()
        own = own + out_recv[1].astype(F32)
        for piece in rs_pieces:
            reduce(2, piece, far).wait_recv()
            low = piece.start
            out_ref[piece, :] = (
                own[low : low + quarter] + out_recv[2, piece].astype(F32)
            ).astype(BF16)
    else:
        for step in range(1, n_mp):
            peer = lax.rem(me + step, n_mp)
            out_send[step] = share(peer).astype(BF16)
            send = remote(
                out_send.at[step], out_recv.at[step], rs_send.at[step, 0], rs_recv.at[step, 0], "mp", peer
            )
            send.start()
            sends.append(send)
        own = share(me) + xg[me].astype(F32)
        for step in range(1, n_mp):
            remote(
                out_send.at[step], out_recv.at[step], rs_send.at[step, 0], rs_recv.at[step, 0], "mp", me
            ).wait_recv()
            own = own + out_recv[step].astype(F32)
        out_ref[...] = own.astype(BF16)

    for send in sends:
        send.wait_send()

    def drain(b):
        for which in range(2):
            for c in range(2):
                to_right = (b == spot) | (b == spot - 1) if hop else b <= spot
                to_left = (b == spot) | (b == spot + 1) if hop else b >= spot

                @pl.when(has_right & to_right)
                def _():
                    block(1, which, b, c, spot + 1).wait_send()

                @pl.when(has_left & to_left)
                def _():
                    block(0, which, b, c, spot - 1).wait_send()

                if hop:

                    @pl.when(ends & (b == spot))
                    def _():
                        block(2, which, b, c, n_seq - 1 - spot).wait_send()

    each(n_seq, drain)


def per_device(n_mp, n_seq, x, gain, wq, wk, wv, softness, wo):
    rows, part = x.shape
    features, head_cols = wq.shape
    span_rows = n_seq if n_seq > UNROLL_LIMIT else 1
    any_space = pl.BlockSpec(memory_space=pl.ANY)
    vmem = pl.BlockSpec(memory_space=pltpu.VMEM)
    slots = max(n_mp, 3)
    return pl.pallas_call(
        functools.partial(kernel, n_mp, n_seq),
        out_shape=jax.ShapeDtypeStruct((rows, part), BF16),
        in_specs=[
            pl.BlockSpec(memory_space=pltpu.SMEM),
            any_space, vmem, any_space, any_space, any_space, any_space,
        ],
        out_specs=vmem,
        scratch_shapes=[
            pltpu.VMEM((n_mp, rows, part), BF16),
            pltpu.VMEM((features, head_cols), BF16),
            pltpu.VMEM((features, head_cols), BF16),
            pltpu.VMEM((features, head_cols), BF16),
            pltpu.VMEM((head_cols, features), BF16),
            pltpu.VMEM((rows, features), BF16),
            pltpu.VMEM((rows, head_cols), BF16),
            pltpu.VMEM((2, n_seq, rows, head_cols), BF16),
            pltpu.VMEM((span_rows, rows, rows), F32),
            pltpu.VMEM((rows, head_cols), BF16),
            pltpu.VMEM((slots, rows, part), BF16),
            pltpu.VMEM((slots, rows, part), BF16),
            pltpu.SemaphoreType.DMA((4,)),
            pltpu.SemaphoreType.DMA,
            pltpu.SemaphoreType.DMA((slots, 2)),
            pltpu.SemaphoreType.DMA((slots, 2)),
            pltpu.SemaphoreType.DMA((3, 2, n_seq, 2)),
            pltpu.SemaphoreType.DMA((2, n_seq, 2)),
            pltpu.SemaphoreType.DMA((slots, RS_PIECES)),
            pltpu.SemaphoreType.DMA((slots, RS_PIECES)),
        ],
        compiler_params=pltpu.CompilerParams(collective_id=0, has_side_effects=True),
    )(softness, x, gain.reshape(1, features), wq, wk, wv, wo)


def solution(mesh):
    return jax.shard_map(
        functools.partial(per_device, mesh.shape["mp"], mesh.shape["seq"]),
        mesh=mesh,
        in_specs=(
            P(("groups", "seq"), "mp"),
            P(),
            P(None, "mp"),
            P(None, "mp"),
            P(None, "mp"),
            P("mp"),
            P("mp", None),
        ),
        out_specs=P(("groups", "seq"), "mp"),
        check_vma=False,
    )
```

```python
import functools
import math

import jax
import jax.numpy as jnp
from jax import lax
from jax.experimental import pallas as pl
from jax.experimental.pallas import tpu as pltpu
from jax.sharding import PartitionSpec as P

MESH = pl.DeviceIdType.MESH
F32 = jnp.float32
BF16 = jnp.bfloat16
UNROLL_LIMIT = 8
RS_PIECES = 2


def remote(src, dst, send_sem, recv_sem, axis, index):
    return pltpu.make_async_remote_copy(
        src_ref=src,
        dst_ref=dst,
        send_sem=send_sem,
        recv_sem=recv_sem,
        device_id={axis: index},
        device_id_type=MESH,
    )


def each(count, body):
    if count <= UNROLL_LIMIT:
        for i in range(count):
            body(i)
    else:
        lax.fori_loop(0, count, lambda i, c: (body(i), c)[1], 0)


def kernel(
    n_mp,
    n_seq,
    softness_ref,
    x_hbm,
    gain_ref,
    wq_hbm,
    wk_hbm,
    wv_hbm,
    wo_hbm,
    out_ref,
    xg,
    wq,
    wk,
    wv,
    wo,
    normed,
    q_ref,
    kv,
    scores,
    heads,
    out_send,
    out_recv,
    w_sem,
    x_sem,
    xg_send,
    xg_recv,
    kv_send,
    kv_recv,
    rs_send,
    rs_recv,
):
    me = lax.axis_index("mp")
    spot = lax.axis_index("seq")
    rows, part = x_hbm.shape
    head_cols = wq_hbm.shape[1]
    groups = softness_ref.shape[0]
    span = head_cols // groups
    paired = n_mp == 4
    has_left = spot > 0
    has_right = spot < n_seq - 1
    hop = n_seq == 4
    ends = (spot == 0) | (spot == n_seq - 1)

    own_x = pltpu.make_async_copy(x_hbm, xg.at[me], x_sem)
    own_x.start()
    loads = [
        pltpu.make_async_copy(src, dst, w_sem.at[i])
        for i, (src, dst) in enumerate(((wk_hbm, wk), (wv_hbm, wv), (wq_hbm, wq), (wo_hbm, wo)))
    ]
    for load in loads:
        load.start()

    barrier = pltpu.get_barrier_semaphore()
    for step in range(1, n_mp):
        pl.semaphore_signal(
            barrier, inc=1, device_id={"mp": lax.rem(me + step, n_mp)}, device_id_type=MESH
        )

    @pl.when(has_left)
    def _():
        pl.semaphore_signal(barrier, inc=1, device_id={"seq": spot - 1}, device_id_type=MESH)

    @pl.when(has_right)
    def _():
        pl.semaphore_signal(barrier, inc=1, device_id={"seq": spot + 1}, device_id_type=MESH)

    greeted = n_mp - 1 + has_left.astype(jnp.int32) + has_right.astype(jnp.int32)
    if hop:

        @pl.when(ends)
        def _():
            pl.semaphore_signal(
                barrier, inc=1, device_id={"seq": n_seq - 1 - spot}, device_id_type=MESH
            )

        greeted = greeted + ends.astype(jnp.int32)
    pl.semaphore_wait(barrier, greeted)

    half = rows // 2
    pieces = [pl.ds(0, half), pl.ds(half, half)]
    near = me + 1 - 2 * lax.rem(me, 2)
    far = lax.rem(me + 2, n_mp)
    cross = lax.rem(near + 2, n_mp)
    sends = []

    def gather(lane, c, source, target):
        slot = xg.at[source, pieces[c]]
        return remote(slot, slot, xg_send.at[lane, c], xg_recv.at[lane, c], "mp", target)

    if paired:
        for lane, peer in ((0, far), (1, near)):
            for c, piece in enumerate(pieces):
                send = remote(
                    x_hbm.at[piece], xg.at[me, piece],
                    xg_send.at[lane, c], xg_recv.at[lane, c], "mp", peer,
                )
                send.start()
                sends.append(send)
    else:
        for c, piece in enumerate(pieces):
            for step in range(1, n_mp):
                send = remote(
                    x_hbm.at[piece], xg.at[me, piece],
                    xg_send.at[step, c], xg_recv.at[step, c], "mp", lax.rem(me + step, n_mp),
                )
                send.start()
                sends.append(send)
    own_x.wait()

    def relay_far(c):
        if paired:
            gather(0, c, far, far).wait_recv()
            relay = gather(2, c, far, near)
            relay.start()
            sends.append(relay)

    def gathered(c):
        if paired:
            gather(1, c, near, near).wait_recv()
            gather(2, c, cross, near).wait_recv()
        else:
            for step in range(1, n_mp):
                source = lax.rem(me - step + n_mp, n_mp)
                gather(step, c, source, source).wait_recv()

    features = n_mp * part

    def normalize(c):
        piece = pieces[c]
        total = jnp.zeros((half, 1), F32)
        for j in range(n_mp):
            total = total + jnp.sum(xg[j, piece, :].astype(F32), axis=-1, keepdims=True)
        average = total / features
        square = jnp.zeros((half, 1), F32)
        for j in range(n_mp):
            off = xg[j, piece, :].astype(F32) - average
            square = square + jnp.sum(off * off, axis=-1, keepdims=True)
        inverse = lax.rsqrt(square / features + 1e-05)
        for j in range(n_mp):
            cols = pl.ds(j * part, part)
            off = xg[j, piece, :].astype(F32) - average
            normed[piece, cols] = (off * inverse * gain_ref[:, cols]).astype(BF16)

    def block(way, which, owner, c, target):
        slot = kv.at[which, owner, pieces[c]]
        return remote(
            slot, slot, kv_send.at[way, which, owner, c], kv_recv.at[which, owner, c], "seq", target
        )

    def project(which, weight, c):
        kv[which, spot, pieces[c]] = jnp.dot(
            normed[pieces[c], :], weight[...], preferred_element_type=F32
        ).astype(BF16)
        launch(which, c)

    def launch(which, c):
        @pl.when(has_right)
        def _():
            block(1, which, spot, c, spot + 1).start()

        @pl.when(has_left)
        def _():
            block(0, which, spot, c, spot - 1).start()

        if hop:

            @pl.when(ends)
            def _():
                block(2, which, spot, c, n_seq - 1 - spot).start()

    relay_far(0)
    gathered(0)
    normalize(0)
    relay_far(1)
    loads[0].wait()
    project(0, wk, 0)
    gathered(1)
    normalize(1)
    project(0, wk, 1)
    loads[1].wait()
    kv[1, spot] = jnp.dot(normed[...], wv[...], preferred_element_type=F32).astype(BF16)
    for c in range(2):
        launch(1, c)
    loads[2].wait()
    q_ref[...] = jnp.dot(normed[...], wq[...], preferred_element_type=F32).astype(BF16)

    def take(which, step, c, forward):
        before = spot - step
        after = spot + step

        @pl.when(before >= 0)
        def _():
            block(1, which, before, c, before).wait_recv()
            if forward:

                @pl.when(has_right)
                def _():
                    block(1, which, before, c, spot + 1).start()

        @pl.when(after < n_seq)
        def _():
            block(0, which, after, c, after).wait_recv()
            if forward:

                @pl.when(has_left)
                def _():
                    block(0, which, after, c, spot - 1).start()

    if hop:
        for which in range(2):
            for c in range(2):
                take(which, 1, c, True)
        for step in (2, 3):
            for c in range(2):
                take(0, step, c, False)

        def last_values():
            for step in (2, 3):
                for c in range(2):
                    take(1, step, c, False)

    else:

        def chain(i):
            for c in range(2):
                for which in range(2):
                    take(which, i + 1, c, True)

        each(n_seq - 1, chain)

        def last_values():
            pass

    if n_seq <= UNROLL_LIMIT:
        sums, chances = [], []
        for h in range(groups):
            cols = pl.ds(h * span, span)
            keys = kv[0, :, :, cols].reshape(n_seq * rows, span)
            s = lax.dot_general(
                q_ref[:, cols], keys, (((1,), (1,)), ((), ())), preferred_element_type=F32
            ) * (softness_ref[h] / math.sqrt(span))
            top = jnp.max(s, axis=-1, keepdims=True)
            w = jnp.exp(s - top)
            sums.append(jnp.sum(w, axis=-1, keepdims=True))
            chances.append(w.astype(BF16))
        last_values()
        for h in range(groups):
            cols = pl.ds(h * span, span)
            values = kv[1, :, :, cols].reshape(n_seq * rows, span)
            mixed = jnp.dot(chances[h], values, preferred_element_type=F32)
            heads[:, cols] = (mixed / sums[h]).astype(BF16)
    else:
        for h in range(groups):
            cols = pl.ds(h * span, span)
            factor = softness_ref[h] / math.sqrt(span)

            def first(b, top):
                s = lax.dot_general(
                    q_ref[:, cols], kv[0, b, :, cols], (((1,), (1,)), ((), ())),
                    preferred_element_type=F32,
                ) * factor
                scores[b] = s
                return jnp.maximum(top, jnp.max(s, axis=-1, keepdims=True))

            top = lax.fori_loop(0, n_seq, first, jnp.full((rows, 1), -jnp.inf, F32))

            def second(b, state):
                summed, mixed = state
                w = jnp.exp(scores[b] - top)
                mixed = mixed + jnp.dot(
                    w.astype(BF16), kv[1, b, :, cols], preferred_element_type=F32
                )
                return summed + jnp.sum(w, axis=-1, keepdims=True), mixed

            summed, mixed = lax.fori_loop(
                0, n_seq, second, (jnp.zeros((rows, 1), F32), jnp.zeros((rows, span), F32))
            )
            heads[:, cols] = (mixed / summed).astype(BF16)

    loads[3].wait()
    rs_pieces = [pl.ds(i * (rows // RS_PIECES), rows // RS_PIECES) for i in range(RS_PIECES)]

    def share(owner):
        cols = pl.ds(pl.multiple_of(owner * part, part), part)
        return jnp.dot(heads[...], wo[:, cols], preferred_element_type=F32)

    if paired:
        quarter = rows // len(rs_pieces)

        def reduce(lane, piece, target):
            return remote(
                out_send.at[lane, piece], out_recv.at[lane, piece],
                rs_send.at[lane, piece.start // quarter], rs_recv.at[lane, piece.start // quarter],
                "mp", target,
            )

        out_send[0] = share(cross).astype(BF16)
        for piece in rs_pieces:
            send = reduce(0, piece, near)
            send.start()
            sends.append(send)
        for_far = share(far)
        for piece in rs_pieces:
            reduce(0, piece, near).wait_recv()
            low = piece.start
            out_send[2, piece] = (
                for_far[low : low + quarter] + out_recv[0, piece].astype(F32)
            ).astype(BF16)
            send = reduce(2, piece, far)
            send.start()
            sends.append(send)
        out_send[1] = share(near).astype(BF16)
        for piece in rs_pieces:
            send = reduce(1, piece, near)
            send.start()
            sends.append(send)
        own = share(me) + xg[me].astype(F32)
        for piece in rs_pieces:
            reduce(1, piece, near).wait_recv()
        own = own + out_recv[1].astype(F32)
        for piece in rs_pieces:
            reduce(2, piece, far).wait_recv()
            low = piece.start
            out_ref[piece, :] = (
                own[low : low + quarter] + out_recv[2, piece].astype(F32)
            ).astype(BF16)
    else:
        for step in range(1, n_mp):
            peer = lax.rem(me + step, n_mp)
            out_send[step] = share(peer).astype(BF16)
            send = remote(
                out_send.at[step], out_recv.at[step], rs_send.at[step, 0], rs_recv.at[step, 0], "mp", peer
            )
            send.start()
            sends.append(send)
        own = share(me) + xg[me].astype(F32)
        for step in range(1, n_mp):
            remote(
                out_send.at[step], out_recv.at[step], rs_send.at[step, 0], rs_recv.at[step, 0], "mp", me
            ).wait_recv()
            own = own + out_recv[step].astype(F32)
        out_ref[...] = own.astype(BF16)

    for send in sends:
        send.wait_send()

    def drain(b):
        for which in range(2):
            for c in range(2):
                to_right = (b == spot) | (b == spot - 1) if hop else b <= spot
                to_left = (b == spot) | (b == spot + 1) if hop else b >= spot

                @pl.when(has_right & to_right)
                def _():
                    block(1, which, b, c, spot + 1).wait_send()

                @pl.when(has_left & to_left)
                def _():
                    block(0, which, b, c, spot - 1).wait_send()

                if hop:

                    @pl.when(ends & (b == spot))
                    def _():
                        block(2, which, b, c, n_seq - 1 - spot).wait_send()

    each(n_seq, drain)


def per_device(n_mp, n_seq, x, gain, wq, wk, wv, softness, wo):
    rows, part = x.shape
    features, head_cols = wq.shape
    span_rows = n_seq if n_seq > UNROLL_LIMIT else 1
    any_space = pl.BlockSpec(memory_space=pl.ANY)
    vmem = pl.BlockSpec(memory_space=pltpu.VMEM)
    slots = max(n_mp, 3)
    return pl.pallas_call(
        functools.partial(kernel, n_mp, n_seq),
        out_shape=jax.ShapeDtypeStruct((rows, part), BF16),
        in_specs=[
            pl.BlockSpec(memory_space=pltpu.SMEM),
            any_space, vmem, any_space, any_space, any_space, any_space,
        ],
        out_specs=vmem,
        scratch_shapes=[
            pltpu.VMEM((n_mp, rows, part), BF16),
            pltpu.VMEM((features, head_cols), BF16),
            pltpu.VMEM((features, head_cols), BF16),
            pltpu.VMEM((features, head_cols), BF16),
            pltpu.VMEM((head_cols, features), BF16),
            pltpu.VMEM((rows, features), BF16),
            pltpu.VMEM((rows, head_cols), BF16),
            pltpu.VMEM((2, n_seq, rows, head_cols), BF16),
            pltpu.VMEM((span_rows, rows, rows), F32),
            pltpu.VMEM((rows, head_cols), BF16),
            pltpu.VMEM((slots, rows, part), BF16),
            pltpu.VMEM((slots, rows, part), BF16),
            pltpu.SemaphoreType.DMA((4,)),
            pltpu.SemaphoreType.DMA,
            pltpu.SemaphoreType.DMA((slots, 2)),
            pltpu.SemaphoreType.DMA((slots, 2)),
            pltpu.SemaphoreType.DMA((3, 2, n_seq, 2)),
            pltpu.SemaphoreType.DMA((2, n_seq, 2)),
            pltpu.SemaphoreType.DMA((slots, RS_PIECES)),
            pltpu.SemaphoreType.DMA((slots, RS_PIECES)),
        ],
        compiler_params=pltpu.CompilerParams(collective_id=0, has_side_effects=True),
    )(softness, x, gain.reshape(1, features), wq, wk, wv, wo)


def solution(mesh):
    return jax.shard_map(
        functools.partial(per_device, mesh.shape["mp"], mesh.shape["seq"]),
        mesh=mesh,
        in_specs=(
            P(("groups", "seq"), "mp"),
            P(),
            P(None, "mp"),
            P(None, "mp"),
            P(None, "mp"),
            P("mp"),
            P("mp", None),
        ),
        out_specs=P(("groups", "seq"), "mp"),
        check_vma=False,
    )
```
